128 devices in a mesh: replica: 4 (over y_lo, core), dp: 32 (over z, x, y_hi).
Axes of the slice: x: 4, y: 4 (y_hi: 2, y_lo: 2; y = y_hi * 2 + y_lo), z: 4, core: 2. Of those that a mesh axis runs over, the one named last changes fastest.
Arguments:
- features: bfloat16 [12288, 256], P('dp'), may hold values from -160 to 160
- prototypes: bfloat16 [256, 131072], P(None, ('replica', 'dp')), may hold values from -120 to 120
Outputs:
- codes: bfloat16 [12288, 131072], P('dp', 'replica')
The draws below stay inside these ranges and needn't reach their ends.
All inputs are finite; a program needn't handle non-finite values.
Results may differ from the reference program's by a relative error of at most 0.0058.
Values may be sent and summed in bfloat16 or wider, within the bound.
A program may use at most 192 MiB of HBM per device.

```python
import math
import jax
import jax.numpy as jnp
from jax import lax

D = 256
PROTOS = 131072
ITERS = 3
BATCH = 12288


cluster_count = 16


def cluster_directions(key):
    return jnp.clip(jax.random.normal(jax.random.fold_in(key, 7), (cluster_count, D), jnp.float32), -4.0, 4.0)


def draw_features(key, part):
    directions = cluster_directions(key)
    first_pick = jax.random.randint(jax.random.fold_in(key, 14), (BATCH,), 0, cluster_count)
    second_pick = jax.random.randint(jax.random.fold_in(key, 15), (BATCH,), 0, cluster_count)
    membership = jnp.minimum(first_pick, second_pick)
    own_direction = directions[membership]
    jitter = jnp.clip(jax.random.normal(jax.random.fold_in(key, 11), (BATCH, D), jnp.float32), -4.0, 4.0)
    loading = jax.random.uniform(jax.random.fold_in(key, 12), (BATCH, 1), jnp.float32, 0.0, 2.0)
    scales = jnp.exp(jax.random.uniform(jax.random.fold_in(key, 13), (BATCH, 1), jnp.float32, 0.0, math.log(10.0)))
    return (scales * (jitter + loading * own_direction)).astype(jnp.bfloat16)


def draw_prototypes(key, part):
    directions = cluster_directions(key)
    membership = jax.random.randint(jax.random.fold_in(key, 24), (PROTOS,), 0, cluster_count)
    own_direction = directions[membership].T
    jitter = jnp.clip(jax.random.normal(jax.random.fold_in(key, 21), (D, PROTOS), jnp.float32), -4.0, 4.0)
    column_tilt = jax.random.uniform(jax.random.fold_in(key, 22), (1, PROTOS), jnp.float32, -1.5, 1.5)
    scales = jnp.exp(jax.random.uniform(jax.random.fold_in(key, 23), (1, PROTOS), jnp.float32, 0.0, math.log(10.0)))
    return (scales * (jitter + column_tilt * own_direction)).astype(jnp.bfloat16)


def setup_inputs(seed: int = 0) -> dict:
    key_of = jax.random.split(jax.random.key(seed), 3)
    features = draw_features(jax.random.fold_in(key_of[2], 71), 0)
    prototypes = draw_prototypes(jax.random.fold_in(key_of[2], 71), 0)
    return {"features": features, "prototypes": prototypes}


epsilon = 1e-06
sharpness_divisor = 0.07

def unit_rows(values):
    return values * lax.rsqrt(lax.optimization_barrier(jnp.sum(values * values, axis=1, keepdims=True)) + epsilon)

def unit_columns(values):
    return values * lax.rsqrt(lax.optimization_barrier(jnp.sum(values * values, axis=0, keepdims=True)) + epsilon)

def exponentials(normalised_embeddings, column_block):
    tempered_scores = unit_columns(column_block.astype(jnp.float32)).astype(jnp.bfloat16)
    scores = jnp.dot(normalised_embeddings, tempered_scores, preferred_element_type=jnp.float32)
    return jnp.exp(scores / sharpness_divisor).astype(jnp.bfloat16)

def reference(features, prototypes):
    normalised_embeddings = unit_rows(features.astype(jnp.float32)).astype(jnp.bfloat16)
    block_width = min(PROTOS, 4096)
    block_count = PROTOS // block_width
    stacked = prototypes.reshape(D, block_count, block_width).transpose(1, 0, 2)

    def make_block(column_block):
        return exponentials(normalised_embeddings, column_block)
    kernel_blocks = lax.map(make_block, stacked)
    row_scale_factors = jnp.ones((BATCH,), jnp.float32)
    cols_scale = jnp.ones((block_count, block_width), jnp.float32)
    for iteration in range(ITERS):
        rounded_rows = row_scale_factors.astype(jnp.bfloat16)

        def column_totals(block):
            return jnp.dot(rounded_rows, block, preferred_element_type=jnp.float32)
        cols_scale = 1.0 / lax.map(column_totals, kernel_blocks)
        rounded_cols = cols_scale.astype(jnp.bfloat16)

        def row_terms(pair):
            return jnp.dot(pair[0], pair[1], preferred_element_type=jnp.float32)
        row_scale_factors = 1.0 / lax.optimization_barrier(jnp.sum(lax.map(row_terms, (kernel_blocks, rounded_cols)), axis=0))
    codes = (PROTOS * kernel_blocks.astype(jnp.float32) * row_scale_factors[None, :, None] * cols_scale[:, None, :]).astype(jnp.bfloat16)
    return codes.transpose(1, 0, 2).reshape(BATCH, PROTOS)
```

```python
import functools

import jax
import jax.numpy as jnp
from jax import lax
from jax.experimental import pallas as pl
from jax.experimental.pallas import tpu as pltpu
from jax.sharding import PartitionSpec as P

PROTOS = 131072
ITERS = 3
epsilon = 1e-06
log2_scale = 1.4426950408889634 / 0.07

f32, bf16 = jnp.float32, jnp.bfloat16
ROWS, COLS = 3072, 4096
DX = (0, 1, 3, 2)
FEATURE_PEERS = [(k, d) for d in (0, 1, 3, 2) for k in (0, 1) if (k, d) != (0, 0)]
PLANE = [(a, b) for a in range(4) for b in range(4) if (a, b) != (0, 0)]
C_PEERS = [(a, b) for a in (0, 2) for b in range(4) if (a, b) != (0, 0)]


def place():
    rep, dp = lax.axis_index("replica"), lax.axis_index("dp")
    return dp // 8, lax.rem(dp // 2, 4), lax.rem(dp, 2), rep // 2, lax.rem(rep, 2)


def at(z, x, y, c):
    return {"replica": lax.rem(y, 2) * 2 + c, "dp": z * 8 + x * 2 + y // 2}


def up(v, d):
    return lax.rem(v + d, 4)


def center(
    feat_ref,
    proto_ref,
    gath,
    c_out,
    r_out,
    f_out,
    F,
    W,
    K,
    cm,
    rm,
    csend,
    crecv,
    rpart,
    rs_recv,
    ysend,
    yz_recv,
    rfull,
    c_all,
    feat_sem,
    twin_sem,
    xg_sem,
    zb_sem,
    ya_sem,
    yb_sem,
    za_sem,
    xb_sem,
    col_sem,
    half_sem,
    yz_sem,
    full_sem,
    call_sem,
    local_sem,
):
    z, x, h, l, c = place()
    y = h * 2 + l
    m0 = z * 2 + h
    xp, xm, xo = at(z, up(x, 1), y, c), at(z, up(x, 3), y, c), up(x, 2)
    zp, zm = at(up(z, 1), x, y, c), at(up(z, 3), x, y, c)
    twin = at(z, x, y, 1 - c)
    yo = at(z, x, up(y, 2), c)

    barrier = pltpu.get_barrier_semaphore()
    peers = [at(z, up(x, d), y, c) for d in (1, 2, 3)]
    peers += [at(up(z, b), x, up(y, a), c) for a, b in PLANE] + [twin]
    for p in peers:
        pl.semaphore_signal(barrier, inc=1, device_id=p, device_id_type=pl.DeviceIdType.MESH)

    fv = feat_ref[...].astype(f32)
    fn = (fv * lax.rsqrt(jnp.sum(fv * fv, axis=1, keepdims=True) + epsilon)).astype(bf16)
    f_out[...] = fn
    F[pl.ds(pl.multiple_of(m0 * 384, 384), 384), :] = fn
    pv = proto_ref[...].astype(f32)
    W[x] = (pv * lax.rsqrt(jnp.sum(pv * pv, axis=0, keepdims=True) + epsilon)).astype(bf16)

    pl.semaphore_wait(barrier, len(peers))
    sends = []

    def remote(src, dst, sems, idx, dev):
        return pltpu.make_async_remote_copy(
            src_ref=src,
            dst_ref=dst,
            send_sem=sems.at[0, idx],
            recv_sem=sems.at[1, idx],
            device_id=dev,
            device_id_type=pl.DeviceIdType.MESH,
        )

    def send(src, dst, sems, idx, dev):
        cp = remote(src, dst, sems, idx, dev)
        cp.start()
        sends.append(cp)

    def arrived(ref, sems, idx):
        remote(ref, ref, sems, idx, twin).wait_recv()

    def g(zz, xx, hh, lo, n):
        return gath.at[zz * 8 + xx * 2 + hh, pl.ds(lo, n)]

    def xh(xx, k):
        return W.at[xx, pl.ds(k * 128, 128)]

    send(xh(x, 0), xh(x, 0), xg_sem, 0, xp)
    send(xh(x, 1), xh(x, 1), xg_sem, 2, xm)
    send(xh(x, 1), xh(x, 1), xg_sem, 1, xp)
    send(xh(x, 0), xh(x, 0), xg_sem, 3, xm)

    def fpart(zz, hh, cc):
        return F.at[pl.ds(pl.multiple_of((zz * 2 + hh) * 384 + cc * 192, 64), 192)]

    mine = fpart(z, h, c)
    for i, (k, d) in enumerate(FEATURE_PEERS):
        send(mine, mine, feat_sem, i, at(up(z, d), x, 3 - y if k else y, c))

    def zq(zz, q):
        return g(zz, x, h, 128 + q * 64, 64)

    def wq(q):
        return W.at[x, pl.ds(128 + q * 64, 64)]

    send(wq(0), zq(z, 0), zb_sem, 0, zp)
    send(wq(1), zq(z, 1), zb_sem, 2, zm)
    send(wq(1), zq(z, 1), zb_sem, 1, zp)
    send(wq(0), zq(z, 0), zb_sem, 3, zm)

    locals_ = []

    def keep(xx, i):
        cp = pltpu.make_async_copy(W.at[xx], gath.at[z * 8 + xx * 2 + h], local_sem.at[i])
        cp.start()
        locals_.append(cp)

    keep(x, 0)

    for i, (k, d) in enumerate(FEATURE_PEERS):
        part = fpart(up(z, 4 - d), 1 - h if k else h, c)
        arrived(part, feat_sem, i)
        send(part, part, twin_sem, i, twin)

    def b_forward():
        arrived(zq(up(z, 3), 0), zb_sem, 0)
        send(zq(up(z, 3), 0), zq(up(z, 3), 0), zb_sem, 4, zp)
        arrived(zq(up(z, 1), 1), zb_sem, 2)
        send(zq(up(z, 1), 1), zq(up(z, 1), 1), zb_sem, 5, zm)

    def hb(zz, xx, hh):
        return g(zz, xx, hh, 128, 128)

    def ha(zz, xx, hh):
        return g(zz, xx, hh, 0, 128)

    def yb0():
        send(W.at[x, pl.ds(128, 128)], hb(z, x, h), yb_sem, 0, yo)

    def b_rest():
        arrived(zq(up(z, 3), 1), zb_sem, 1)
        arrived(zq(up(z, 1), 0), zb_sem, 3)
        arrived(zq(up(z, 2), 0), zb_sem, 4)
        arrived(zq(up(z, 2), 1), zb_sem, 5)

    def yb(i):
        zz = up(z, DX[i])
        send(hb(zz, x, h), hb(zz, x, h), yb_sem, i, yo)

    def ya(i):
        xx = up(x, DX[i])
        send(W.at[xx, pl.ds(0, 128)], ha(z, xx, h), ya_sem, i, yo)

    def za_ref(zz, i):
        return ha(zz, up(x, DX[i % 4]), h if i < 4 else 1 - h)

    def za(i):
        if i >= 4:
            arrived(za_ref(z, i), ya_sem, i - 4)
            src = za_ref(z, i)
        else:
            src = W.at[up(x, DX[i]), pl.ds(0, 128)]
        send(src, za_ref(z, i), za_sem, i, zp)
        send(src, za_ref(z, i), za_sem, 8 + i, zm)

    def za_forward(i):
        lo, hi = za_ref(up(z, 3), i), za_ref(up(z, 1), i)
        if i % 2 == 0:
            arrived(lo, za_sem, i)
            send(lo, lo, za_sem, 16 + i, zp)
        else:
            arrived(hi, za_sem, 8 + i)
            send(hi, hi, za_sem, 16 + i, zm)

    def za_rest(i):
        if i % 2 == 0:
            arrived(za_ref(up(z, 1), i), za_sem, 8 + i)
        else:
            arrived(za_ref(up(z, 3), i), za_sem, i)
        arrived(za_ref(up(z, 2), i), za_sem, 16 + i)

    XB = [(1, 0), (3, 0), (2, 0), (0, 1), (1, 1), (3, 1), (2, 1)]

    def xb_ref(xx, j):
        d, o = XB[j]
        return hb(up(z, d), xx, 1 - h if o else h)

    def xb(j):
        d, o = XB[j]
        if o:
            arrived(xb_ref(x, j), yb_sem, DX.index(d))
        send(xb_ref(x, j), xb_ref(x, j), xb_sem, j, xp)
        send(xb_ref(x, j), xb_ref(x, j), xb_sem, 7 + j, xm)

    def xb_forward(j):
        lo, hi = xb_ref(up(x, 3), j), xb_ref(up(x, 1), j)
        if j % 2 == 0:
            arrived(lo, xb_sem, j)
            send(lo, lo, xb_sem, 14 + j, xp)
        else:
            arrived(hi, xb_sem, 7 + j)
            send(hi, hi, xb_sem, 14 + j, xm)

    def xb_rest(j):
        if j % 2 == 0:
            arrived(xb_ref(up(x, 1), j), xb_sem, 7 + j)
        else:
            arrived(xb_ref(up(x, 3), j), xb_sem, j)
        arrived(xb_ref(up(x, 2), j), xb_sem, 14 + j)

    def many(fn, ids):
        return [functools.partial(fn, i) for i in ids]

    steps = [yb0, b_rest] + many(yb, (1, 2, 3)) + many(ya, range(4))
    steps += many(za, range(4)) + many(xb, range(3)) + many(za_forward, range(4)) + many(xb_forward, range(3))
    steps += many(za, range(4, 8)) + many(xb, range(3, 7))
    steps += many(za_forward, range(4, 8)) + many(xb_forward, range(3, 7))
    steps += many(za_rest, range(8)) + many(xb_rest, range(7))

    def pump(n):
        for _ in range(min(n, len(steps))):
            steps.pop(0)()

    def exponentials(d):
        xx = up(x, d)
        w = W.at[xx]

        def body(rb, acc):
            r0 = pl.multiple_of(rb * 512, 512)
            a = F[pl.ds(r0, 512), :]
            parts = []
            for q in range(4):
                s = jnp.dot(a, w[:, q * 256 : (q + 1) * 256], preferred_element_type=f32)
                e = jnp.exp2(s * log2_scale)
                c0 = pl.multiple_of(xx * 1024 + q * 256, 256)
                K[pl.ds(r0, 512), pl.ds(c0, 256)] = e.astype(bf16)
                parts.append(jnp.sum(e.reshape(64, 8, 256), axis=0))
            return acc + jnp.concatenate(parts, axis=1)

        acc = lax.fori_loop(0, ROWS // 512, body, jnp.zeros((8, 1024), f32))
        csend[0, xx] = jnp.sum(acc, axis=0, keepdims=True)

    for i, (k, d) in enumerate(FEATURE_PEERS):
        arrived(fpart(up(z, 4 - d), 1 - h if k else h, 1 - c), twin_sem, i)
    arrived(xh(up(x, 3), 0), xg_sem, 0)
    send(xh(up(x, 3), 0), xh(up(x, 3), 0), xg_sem, 4, xp)
    arrived(xh(up(x, 1), 1), xg_sem, 2)
    send(xh(up(x, 1), 1), xh(up(x, 1), 1), xg_sem, 5, xm)
    b_forward()
    exponentials(0)
    arrived(xh(up(x, 3), 1), xg_sem, 1)
    keep(up(x, 3), 1)
    exponentials(3)
    arrived(xh(up(x, 1), 0), xg_sem, 3)
    keep(up(x, 1), 2)
    exponentials(1)
    arrived(xh(xo, 0), xg_sem, 4)
    arrived(xh(xo, 1), xg_sem, 5)
    keep(xo, 3)
    exponentials(2)

    for t in range(ITERS):
        if t:
            for hf in range(2):
                s = jnp.dot(rm[...], K[:, hf * 2048 : (hf + 1) * 2048], preferred_element_type=f32)
                csend[t, 2 * hf] = s[0:1, 0:1024]
                csend[t, 2 * hf + 1] = s[0:1, 1024:2048]
        for d in (1, 2, 3):
            send(csend.at[t], crecv.at[t, d - 1], col_sem, t * 3 + d - 1, at(z, up(x, d), y, c))
        for d in (1, 2, 3):
            arrived(crecv.at[t, d - 1], col_sem, t * 3 + d - 1)
        cols = 1.0 / (csend[t] + crecv[t, 0] + crecv[t, 1] + crecv[t, 2])
        for u in range(4):
            cm[:, u * 1024 : (u + 1) * 1024] = jnp.broadcast_to(cols[u], (16, 1024)).astype(bf16)
        if t == ITERS - 1:
            c_all[m0] = cols
            for i, (a, b) in enumerate(C_PEERS):
                send(c_all.at[m0], c_all.at[m0], call_sem, i, at(up(z, b), x, up(y, a), c))

        for hf in range(2):
            @pl.loop(0, 3)
            def _(rb):
                r0 = pl.multiple_of(rb * 512, 512)
                s = lax.dot_general(
                    cm[...],
                    K[pl.ds(pl.multiple_of(hf * 1536 + rb * 512, 512), 512), :],
                    (((1,), (1,)), ((), ())),
                    preferred_element_type=f32,
                )
                rpart[t, hf, :, pl.ds(r0, 512)] = s[0:1]

        send(rpart.at[t, 1 - c], rs_recv.at[t], half_sem, t, twin)
        arrived(rs_recv.at[t], half_sem, t)
        ysend[t] = rpart[t, c] + rs_recv[t]
        for i, (a, b) in enumerate(PLANE):
            send(ysend.at[t], yz_recv.at[t, i], yz_sem, t * 15 + i, at(up(z, b), x, up(y, a), c))
        for i in range(15):
            arrived(yz_recv.at[t, i], yz_sem, t * 15 + i)
        total = ysend[t] + jnp.sum(yz_recv[t], axis=0)
        rfull[t, c] = 1.0 / total
        send(rfull.at[t, c], rfull.at[t, c], full_sem, t, twin)
        arrived(rfull.at[t, 1 - c], full_sem, t)
        if t < ITERS - 1:
            for hf in range(2):
                rm[:, hf * 1536 : (hf + 1) * 1536] = jnp.broadcast_to(rfull[t, hf], (16, 1536)).astype(bf16)

    r_out[...] = rfull[ITERS - 1, m0 // 4, :, pl.ds(pl.multiple_of(lax.rem(m0, 4) * 384, 384), 384)]
    pump(len(steps))
    for i, (a, b) in enumerate(C_PEERS):
        arrived(c_all.at[up(z, 4 - b) * 2 + up(y, 4 - a) // 2], call_sem, i)
    c_out[...] = c_all[...]
    for cp in locals_:
        cp.wait()
    for cp in sends:
        cp.wait_send()


NB = 4


def finish(f_ref, w_ref, r_ref, c_ref, o_ref, wb, ob, si, so):
    def fetch(i, s):
        return pltpu.make_async_copy(w_ref.at[i], wb.at[s], si.at[s])

    def write(i, s):
        cols = pl.ds(pl.multiple_of(i * 1024, 1024), 1024)
        return pltpu.make_async_copy(ob.at[s], o_ref.at[:, cols], so.at[s])

    for s in range(NB - 1):
        fetch(s, s).start()

    @pl.loop(0, 32)
    def _(i):
        s = lax.rem(i, NB)

        @pl.when(i + NB - 1 < 32)
        def _():
            fetch(i + NB - 1, lax.rem(i + NB - 1, NB)).start()

        fetch(i, s).wait()

        @pl.when(i >= NB)
        def _():
            write(i - NB, s).wait()

        cols = c_ref[(i // 8) * 2 + lax.rem(i, 2), lax.rem(i // 2, 4)]
        for rb in range(3):
            rows = slice(rb * 128, (rb + 1) * 128)
            sc = jnp.dot(f_ref[rows, :], wb[s], preferred_element_type=f32)
            ob[s, rows, :] = (jnp.exp2(sc * log2_scale) * (r_ref[rows, :] * PROTOS) * cols).astype(bf16)
        write(i, s).start()

    for i in range(32 - NB, 32):
        write(i, i % NB).wait()


def local(features, prototypes):
    vmem, anywhere = pl.BlockSpec(memory_space=pltpu.VMEM), pl.BlockSpec(memory_space=pl.ANY)
    dma = lambda n: pltpu.SemaphoreType.DMA((2, n))
    gathered, cols, rows, normed = pl.pallas_call(
        center,
        name="center",
        out_shape=(
            jax.ShapeDtypeStruct((32, 256, 1024), bf16),
            jax.ShapeDtypeStruct((8, 4, 1, 1024), f32),
            jax.ShapeDtypeStruct((1, 384), f32),
            jax.ShapeDtypeStruct((384, 256), bf16),
        ),
        in_specs=[vmem, vmem],
        out_specs=(anywhere, vmem, vmem, vmem),
        scratch_shapes=[
            pltpu.VMEM((ROWS, 256), bf16),
            pltpu.VMEM((4, 256, 1024), bf16),
            pltpu.VMEM((ROWS, COLS), bf16),
            pltpu.VMEM((16, COLS), bf16),
            pltpu.VMEM((16, ROWS), bf16),
            pltpu.VMEM((ITERS, 4, 1, 1024), f32),
            pltpu.VMEM((ITERS, 3, 4, 1, 1024), f32),
            pltpu.VMEM((ITERS, 2, 1, 1536), f32),
            pltpu.VMEM((ITERS, 1, 1536), f32),
            pltpu.VMEM((ITERS, 1, 1536), f32),
            pltpu.VMEM((ITERS, 15, 1, 1536), f32),
            pltpu.VMEM((ITERS, 2, 1, 1536), f32),
            pltpu.VMEM((8, 4, 1, 1024), f32),
            dma(7),
            dma(7),
            dma(6),
            dma(6),
            dma(4),
            dma(4),
            dma(24),
            dma(21),
            dma(9),
            dma(3),
            dma(45),
            dma(3),
            dma(7),
            pltpu.SemaphoreType.DMA((4,)),
        ],
        compiler_params=pltpu.CompilerParams(
            collective_id=0, has_side_effects=True, vmem_limit_bytes=56 << 20
        ),
    )(features, prototypes)
    return pl.pallas_call(
        finish,
        name="finish",
        out_shape=jax.ShapeDtypeStruct((384, 32768), bf16),
        in_specs=[vmem, anywhere, vmem, vmem],
        out_specs=anywhere,
        scratch_shapes=[
            pltpu.VMEM((NB, 256, 1024), bf16),
            pltpu.VMEM((NB, 384, 1024), bf16),
            pltpu.SemaphoreType.DMA((NB,)),
            pltpu.SemaphoreType.DMA((NB,)),
        ],
        compiler_params=pltpu.CompilerParams(vmem_limit_bytes=56 << 20),
    )(normed, gathered, rows.reshape(384, 1), cols)


def solution(mesh):
    placed = (P("dp", None), P(None, ("replica", "dp")))
    return jax.shard_map(
        local, mesh=mesh, in_specs=placed, out_specs=P("dp", "replica"), check_vma=False
    )
```

```python
import functools

import jax
import jax.numpy as jnp
from jax import lax
from jax.experimental import pallas as pl
from jax.experimental.pallas import tpu as pltpu
from jax.sharding import PartitionSpec as P

PROTOS = 131072
ITERS = 3
epsilon = 1e-06
log2_scale = 1.4426950408889634 / 0.07

f32, bf16 = jnp.float32, jnp.bfloat16
ROWS, COLS = 3072, 4096
DX = (0, 1, 3, 2)
FEATURE_PEERS = [(k, d) for d in (0, 1, 3, 2) for k in (0, 1) if (k, d) != (0, 0)]
PLANE = [(a, b) for a in range(4) for b in range(4) if (a, b) != (0, 0)]
C_PEERS = [(a, b) for a in (0, 2) for b in range(4) if (a, b) != (0, 0)]


def place():
    rep, dp = lax.axis_index("replica"), lax.axis_index("dp")
    return dp // 8, lax.rem(dp // 2, 4), lax.rem(dp, 2), rep // 2, lax.rem(rep, 2)


def at(z, x, y, c):
    return {"replica": lax.rem(y, 2) * 2 + c, "dp": z * 8 + x * 2 + y // 2}


def up(v, d):
    return lax.rem(v + d, 4)


def center(
    feat_ref,
    proto_ref,
    gath,
    c_out,
    r_out,
    f_out,
    F,
    W,
    K,
    cm,
    rm,
    csend,
    crecv,
    rpart,
    rs_recv,
    ysend,
    yz_recv,
    rfull,
    c_all,
    feat_sem,
    twin_sem,
    xg_sem,
    zb_sem,
    ya_sem,
    yb_sem,
    xa_sem,
    za_sem,
    xb_sem,
    col_sem,
    half_sem,
    yz_sem,
    full_sem,
    call_sem,
    local_sem,
):
    z, x, h, l, c = place()
    y = h * 2 + l
    m0 = z * 2 + h
    xp, xm, xo = at(z, up(x, 1), y, c), at(z, up(x, 3), y, c), up(x, 2)
    zp, zm = at(up(z, 1), x, y, c), at(up(z, 3), x, y, c)
    twin = at(z, x, y, 1 - c)
    yo = at(z, x, up(y, 2), c)

    barrier = pltpu.get_barrier_semaphore()
    peers = [at(z, up(x, d), y, c) for d in (1, 2, 3)]
    peers += [at(up(z, b), x, up(y, a), c) for a, b in PLANE] + [twin]
    for p in peers:
        pl.semaphore_signal(barrier, inc=1, device_id=p, device_id_type=pl.DeviceIdType.MESH)

    fv = feat_ref[...].astype(f32)
    fn = (fv * lax.rsqrt(jnp.sum(fv * fv, axis=1, keepdims=True) + epsilon)).astype(bf16)
    f_out[...] = fn
    F[pl.ds(pl.multiple_of(m0 * 384, 384), 384), :] = fn
    pv = proto_ref[...].astype(f32)
    W[x] = (pv * lax.rsqrt(jnp.sum(pv * pv, axis=0, keepdims=True) + epsilon)).astype(bf16)

    pl.semaphore_wait(barrier, len(peers))
    sends = []

    def remote(src, dst, sems, idx, dev):
        return pltpu.make_async_remote_copy(
            src_ref=src,
            dst_ref=dst,
            send_sem=sems.at[0, idx],
            recv_sem=sems.at[1, idx],
            device_id=dev,
            device_id_type=pl.DeviceIdType.MESH,
        )

    def send(src, dst, sems, idx, dev):
        cp = remote(src, dst, sems, idx, dev)
        cp.start()
        sends.append(cp)

    def arrived(ref, sems, idx):
        remote(ref, ref, sems, idx, twin).wait_recv()

    def g(zz, xx, hh, lo, n):
        return gath.at[zz * 8 + xx * 2 + hh, pl.ds(lo, n)]

    def xh(xx, k):
        return W.at[xx, pl.ds(k * 128, 128)]

    send(xh(x, 0), xh(x, 0), xg_sem, 0, xp)
    send(xh(x, 1), xh(x, 1), xg_sem, 2, xm)
    send(xh(x, 1), xh(x, 1), xg_sem, 1, xp)
    send(xh(x, 0), xh(x, 0), xg_sem, 3, xm)

    def fpart(zz, hh, cc):
        return F.at[pl.ds(pl.multiple_of((zz * 2 + hh) * 384 + cc * 192, 64), 192)]

    mine = fpart(z, h, c)
    for i, (k, d) in enumerate(FEATURE_PEERS):
        send(mine, mine, feat_sem, i, at(up(z, d), x, 3 - y if k else y, c))

    def zq(zz, hh, q):
        return g(zz, x, hh, 128 + q * 64, 64)

    def wq(q):
        return W.at[x, pl.ds(128 + q * 64, 64)]

    send(wq(0), zq(z, h, 0), zb_sem, 0, zp)
    send(wq(1), zq(z, h, 1), zb_sem, 2, zm)
    send(wq(1), zq(z, h, 1), zb_sem, 1, zp)
    send(wq(0), zq(z, h, 0), zb_sem, 3, zm)

    locals_ = []

    def keep(xx, i):
        cp = pltpu.make_async_copy(W.at[xx], gath.at[z * 8 + xx * 2 + h], local_sem.at[i])
        cp.start()
        locals_.append(cp)

    keep(x, 0)

    def b_forward():
        arrived(zq(up(z, 3), h, 0), zb_sem, 0)
        send(zq(up(z, 3), h, 0), zq(up(z, 3), h, 0), zb_sem, 4, zp)
        arrived(zq(up(z, 1), h, 1), zb_sem, 2)
        send(zq(up(z, 1), h, 1), zq(up(z, 1), h, 1), zb_sem, 5, zm)

    def b2():
        arrived(hb(z, x, 1 - h), yb_sem, 0)
        for q, i, dev in ((0, 0, zp), (1, 2, zm), (1, 1, zp), (0, 3, zm)):
            send(zq(z, 1 - h, q), zq(z, 1 - h, q), zb_sem, 6 + i, dev)

    def b2_forward():
        arrived(zq(up(z, 3), 1 - h, 0), zb_sem, 6)
        send(zq(up(z, 3), 1 - h, 0), zq(up(z, 3), 1 - h, 0), zb_sem, 10, zp)
        arrived(zq(up(z, 1), 1 - h, 1), zb_sem, 8)
        send(zq(up(z, 1), 1 - h, 1), zq(up(z, 1), 1 - h, 1), zb_sem, 11, zm)

    def hb(zz, xx, hh):
        return g(zz, xx, hh, 128, 128)

    def ha(zz, xx, hh):
        return g(zz, xx, hh, 0, 128)

    def yb0():
        send(W.at[x, pl.ds(128, 128)], hb(z, x, h), yb_sem, 0, yo)

    def b_rest(o):
        hh, k = (1 - h, 6) if o else (h, 0)
        arrived(zq(up(z, 3), hh, 1), zb_sem, k + 1)
        arrived(zq(up(z, 1), hh, 0), zb_sem, k + 3)
        arrived(zq(up(z, 2), hh, 0), zb_sem, k + 4)
        arrived(zq(up(z, 2), hh, 1), zb_sem, k + 5)

    def ya0():
        send(W.at[x, pl.ds(0, 128)], ha(z, x, h), ya_sem, 0, yo)

    def za_ref(zz, i):
        return ha(zz, up(x, DX[i % 4]), h if i < 4 else 1 - h)

    def za(i):
        if i >= 4:
            src = za_ref(z, i)
        else:
            src = W.at[up(x, DX[i]), pl.ds(0, 128)]
        send(src, za_ref(z, i), za_sem, i, zp)
        send(src, za_ref(z, i), za_sem, 8 + i, zm)

    def za_forward(i):
        lo, hi = za_ref(up(z, 3), i), za_ref(up(z, 1), i)
        if i % 2 == 0:
            arrived(lo, za_sem, i)
            send(lo, lo, za_sem, 16 + i, zp)
        else:
            arrived(hi, za_sem, 8 + i)
            send(hi, hi, za_sem, 16 + i, zm)

    XB = [(1, 0), (3, 0), (2, 0), (0, 1), (1, 1), (3, 1), (2, 1)]

    def xb_ref(xx, j):
        d, o = XB[j]
        return hb(up(z, d), xx, 1 - h if o else h)

    def xb(j):
        send(xb_ref(x, j), xb_ref(x, j), xb_sem, j, xp)
        send(xb_ref(x, j), xb_ref(x, j), xb_sem, 7 + j, xm)

    def xb_forward(j):
        lo, hi = xb_ref(up(x, 3), j), xb_ref(up(x, 1), j)
        if j % 2 == 0:
            arrived(lo, xb_sem, j)
            send(lo, lo, xb_sem, 14 + j, xp)
        else:
            arrived(hi, xb_sem, 7 + j)
            send(hi, hi, xb_sem, 14 + j, xm)

    def xb_rest(j):
        if j % 2 == 0:
            arrived(xb_ref(up(x, 1), j), xb_sem, 7 + j)
        else:
            arrived(xb_ref(up(x, 3), j), xb_sem, j)
        arrived(xb_ref(up(x, 2), j), xb_sem, 14 + j)

    def aq(xx, q):
        return g(z, xx, 1 - h, q * 64, 64)

    def xa():
        arrived(ha(z, x, 1 - h), ya_sem, 0)
        for q, i, dev in ((0, 0, xp), (1, 2, xm), (1, 1, xp), (0, 3, xm)):
            send(aq(x, q), aq(x, q), xa_sem, i, dev)

    def xa_forward():
        arrived(aq(up(x, 3), 0), xa_sem, 0)
        send(aq(up(x, 3), 0), aq(up(x, 3), 0), xa_sem, 4, xp)
        arrived(aq(up(x, 1), 1), xa_sem, 2)
        send(aq(up(x, 1), 1), aq(up(x, 1), 1), xa_sem, 5, xm)

    def xa_rest():
        arrived(aq(up(x, 3), 1), xa_sem, 1)
        arrived(aq(up(x, 1), 0), xa_sem, 3)
        arrived(aq(xo, 0), xa_sem, 4)
        arrived(aq(xo, 1), xa_sem, 5)

    def near(i):
        if i % 2 == 0:
            arrived(za_ref(up(z, 1), i), za_sem, 8 + i)
        else:
            arrived(za_ref(up(z, 3), i), za_sem, i)

    def far(i):
        arrived(za_ref(up(z, 2), i), za_sem, 16 + i)

    def many(fn, ids):
        return [functools.partial(fn, i) for i in ids]

    plan = {
        "start": [yb0, ya0] + many(za, (0,)),
        "k0": [b_forward, b2],
        "k3": [xa],
        "k1": many(za, (1,)),
        "k2": many(za, (2,)) + many(b_rest, (0,)),
        "colx0": [xa_forward] + many(xb, (0, 1)) + [b2_forward],
        "mid0": many(xb_forward, (0,)),
        "yz0": many(za_forward, (0, 1)) + many(za, (3, 4)) + many(b_rest, (1,)) + [xa_rest],
        "colx1": many(xb_forward, (1,)) + many(xb, (2, 3)),
        "mid1": many(xb_forward, (2,)),
        "yz1": many(za_forward, (2, 3)) + many(za, (5, 6)),
        "col2": many(za_forward, (4,)),
        "colx2": many(xb_forward, (3,)) + many(xb, (4, 5, 6)),
        "mid2": many(xb_forward, (4,)),
        "yz2": many(za, (7,)) + many(za_forward, (5, 6)) + many(xb_forward, (5, 6)) + many(za_forward, (7,)),
        "rest": many(near, range(8)) + many(far, range(8)) + many(xb_rest, range(7)),
    }

    def run(point):
        for fn in plan.pop(point, ()):
            fn()

    def exponentials(d):
        xx = up(x, d)
        w = W.at[xx]

        def body(rb, acc):
            r0 = pl.multiple_of(rb * 512, 512)
            a = F[pl.ds(r0, 512), :]
            parts = []
            for q in range(4):
                s = jnp.dot(a, w[:, q * 256 : (q + 1) * 256], preferred_element_type=f32)
                e = jnp.exp2(s * log2_scale)
                c0 = pl.multiple_of(xx * 1024 + q * 256, 256)
                K[pl.ds(r0, 512), pl.ds(c0, 256)] = e.astype(bf16)
                parts.append(jnp.sum(e.reshape(64, 8, 256), axis=0))
            return acc + jnp.concatenate(parts, axis=1)

        acc = lax.fori_loop(0, ROWS // 512, body, jnp.zeros((8, 1024), f32))
        csend[0, xx] = jnp.sum(acc, axis=0, keepdims=True)

    run("start")
    arrived(xh(up(x, 3), 0), xg_sem, 0)
    send(xh(up(x, 3), 0), xh(up(x, 3), 0), xg_sem, 4, xp)
    arrived(xh(up(x, 1), 1), xg_sem, 2)
    send(xh(up(x, 1), 1), xh(up(x, 1), 1), xg_sem, 5, xm)
    for i, (k, d) in enumerate(FEATURE_PEERS):
        part = fpart(up(z, 4 - d), 1 - h if k else h, c)
        arrived(part, feat_sem, i)
        send(part, part, twin_sem, i, twin)
    for i, (k, d) in enumerate(FEATURE_PEERS):
        arrived(fpart(up(z, 4 - d), 1 - h if k else h, 1 - c), twin_sem, i)
    exponentials(0)
    run("k0")
    arrived(xh(up(x, 3), 1), xg_sem, 1)
    keep(up(x, 3), 1)
    run("k3")
    exponentials(3)
    arrived(xh(up(x, 1), 0), xg_sem, 3)
    keep(up(x, 1), 2)
    run("k1")
    exponentials(1)
    arrived(xh(xo, 0), xg_sem, 4)
    arrived(xh(xo, 1), xg_sem, 5)
    keep(xo, 3)
    run("k2")
    exponentials(2)

    for t in range(ITERS):
        if t:
            run("col%d" % t)
            for hf in range(2):
                s = jnp.dot(rm[...], K[:, hf * 2048 : (hf + 1) * 2048], preferred_element_type=f32)
                csend[t, 2 * hf] = s[0:1, 0:1024]
                csend[t, 2 * hf + 1] = s[0:1, 1024:2048]
        for d in (1, 2, 3):
            send(csend.at[t], crecv.at[t, d - 1], col_sem, t * 3 + d - 1, at(z, up(x, d), y, c))
        run("colx%d" % t)
        for d in (1, 2, 3):
            arrived(crecv.at[t, d - 1], col_sem, t * 3 + d - 1)
        cols = 1.0 / (csend[t] + crecv[t, 0] + crecv[t, 1] + crecv[t, 2])
        for u in range(4):
            cm[:, u * 1024 : (u + 1) * 1024] = jnp.broadcast_to(cols[u], (16, 1024)).astype(bf16)
        if t == ITERS - 1:
            c_all[m0] = cols
            for i, (a, b) in enumerate(C_PEERS):
                send(c_all.at[m0], c_all.at[m0], call_sem, i, at(up(z, b), x, up(y, a), c))

        for hf in range(2):
            if hf:
                run("mid%d" % t)

            @pl.loop(0, 3)
            def _(rb):
                r0 = pl.multiple_of(rb * 512, 512)
                s = lax.dot_general(
                    cm[...],
                    K[pl.ds(pl.multiple_of(hf * 1536 + rb * 512, 512), 512), :],
                    (((1,), (1,)), ((), ())),
                    preferred_element_type=f32,
                )
                rpart[t, hf, :, pl.ds(r0, 512)] = s[0:1]

        send(rpart.at[t, 1 - c], rs_recv.at[t], half_sem, t, twin)
        arrived(rs_recv.at[t], half_sem, t)
        ysend[t] = rpart[t, c] + rs_recv[t]
        for i, (a, b) in enumerate(PLANE):
            send(ysend.at[t], yz_recv.at[t, i], yz_sem, t * 15 + i, at(up(z, b), x, up(y, a), c))
        run("yz%d" % t)
        for i in range(15):
            arrived(yz_recv.at[t, i], yz_sem, t * 15 + i)
        total = ysend[t] + jnp.sum(yz_recv[t], axis=0)
        rfull[t, c] = 1.0 / total
        send(rfull.at[t, c], rfull.at[t, c], full_sem, t, twin)
        arrived(rfull.at[t, 1 - c], full_sem, t)
        if t < ITERS - 1:
            for hf in range(2):
                rm[:, hf * 1536 : (hf + 1) * 1536] = jnp.broadcast_to(rfull[t, hf], (16, 1536)).astype(bf16)

    r_out[...] = rfull[ITERS - 1, m0 // 4, :, pl.ds(pl.multiple_of(lax.rem(m0, 4) * 384, 384), 384)]
    run("rest")
    for i, (a, b) in enumerate(C_PEERS):
        arrived(c_all.at[up(z, 4 - b) * 2 + up(y, 4 - a) // 2], call_sem, i)
    c_out[...] = c_all[...]
    for cp in locals_:
        cp.wait()
    for cp in sends:
        cp.wait_send()


NB = 4


def finish(f_ref, w_ref, r_ref, c_ref, o_ref, rcol, wb, ob, si, so):
    def fetch(i, s):
        return pltpu.make_async_copy(w_ref.at[i], wb.at[s], si.at[s])

    def write(i, s):
        cols = pl.ds(pl.multiple_of(i * 1024, 1024), 1024)
        return pltpu.make_async_copy(ob.at[s], o_ref.at[:, cols], so.at[s])

    for s in range(NB - 1):
        fetch(s, s).start()
    rcol[...] = jnp.broadcast_to(r_ref[...] * PROTOS, (8, 384)).T

    @pl.loop(0, 32)
    def _(i):
        s = lax.rem(i, NB)

        @pl.when(i + NB - 1 < 32)
        def _():
            fetch(i + NB - 1, lax.rem(i + NB - 1, NB)).start()

        fetch(i, s).wait()

        @pl.when(i >= NB)
        def _():
            write(i - NB, s).wait()

        cols = c_ref[(i // 8) * 2 + lax.rem(i, 2), lax.rem(i // 2, 4)]
        for rb in range(3):
            rows = slice(rb * 128, (rb + 1) * 128)
            sc = jnp.dot(f_ref[rows, :], wb[s], preferred_element_type=f32)
            ob[s, rows, :] = (jnp.exp2(sc * log2_scale) * rcol[rows, 0:1] * cols).astype(bf16)
        write(i, s).start()

    for i in range(32 - NB, 32):
        write(i, i % NB).wait()


def local(features, prototypes):
    vmem, anywhere = pl.BlockSpec(memory_space=pltpu.VMEM), pl.BlockSpec(memory_space=pl.ANY)
    dma = lambda n: pltpu.SemaphoreType.DMA((2, n))
    gathered, cols, rows, normed = pl.pallas_call(
        center,
        name="center",
        out_shape=(
            jax.ShapeDtypeStruct((32, 256, 1024), bf16),
            jax.ShapeDtypeStruct((8, 4, 1, 1024), f32),
            jax.ShapeDtypeStruct((1, 384), f32),
            jax.ShapeDtypeStruct((384, 256), bf16),
        ),
        in_specs=[vmem, vmem],
        out_specs=(anywhere, vmem, vmem, vmem),
        scratch_shapes=[
            pltpu.VMEM((ROWS, 256), bf16),
            pltpu.VMEM((4, 256, 1024), bf16),
            pltpu.VMEM((ROWS, COLS), bf16),
            pltpu.VMEM((16, COLS), bf16),
            pltpu.VMEM((16, ROWS), bf16),
            pltpu.VMEM((ITERS, 4, 1, 1024), f32),
            pltpu.VMEM((ITERS, 3, 4, 1, 1024), f32),
            pltpu.VMEM((ITERS, 2, 1, 1536), f32),
            pltpu.VMEM((ITERS, 1, 1536), f32),
            pltpu.VMEM((ITERS, 1, 1536), f32),
            pltpu.VMEM((ITERS, 15, 1, 1536), f32),
            pltpu.VMEM((ITERS, 2, 1, 1536), f32),
            pltpu.VMEM((8, 4, 1, 1024), f32),
            dma(7),
            dma(7),
            dma(6),
            dma(12),
            dma(1),
            dma(1),
            dma(6),
            dma(24),
            dma(21),
            dma(9),
            dma(3),
            dma(45),
            dma(3),
            dma(7),
            pltpu.SemaphoreType.DMA((4,)),
        ],
        compiler_params=pltpu.CompilerParams(
            collective_id=0, has_side_effects=True, vmem_limit_bytes=56 << 20
        ),
    )(features, prototypes)
    return pl.pallas_call(
        finish,
        name="finish",
        out_shape=jax.ShapeDtypeStruct((384, 32768), bf16),
        in_specs=[vmem, anywhere, vmem, vmem],
        out_specs=anywhere,
        scratch_shapes=[
            pltpu.VMEM((384, 8), f32),
            pltpu.VMEM((NB, 256, 1024), bf16),
            pltpu.VMEM((NB, 384, 1024), bf16),
            pltpu.SemaphoreType.DMA((NB,)),
            pltpu.SemaphoreType.DMA((NB,)),
        ],
        compiler_params=pltpu.CompilerParams(vmem_limit_bytes=56 << 20),
    )(normed, gathered, rows, cols)


def solution(mesh):
    placed = (P("dp", None), P(None, ("replica", "dp")))
    return jax.shard_map(
        local, mesh=mesh, in_specs=placed, out_specs=P("dp", "replica"), check_vma=False
    )
```

```python
import functools

import jax
import jax.numpy as jnp
from jax import lax
from jax.experimental import pallas as pl
from jax.experimental.pallas import tpu as pltpu
from jax.sharding import PartitionSpec as P

PROTOS = 131072
ITERS = 3
epsilon = 1e-06
log2_scale = 1.4426950408889634 / 0.07

f32, bf16 = jnp.float32, jnp.bfloat16
ROWS, COLS = 3072, 4096
SPLIT = 2304
DX = (0, 1, 3, 2)
FEATURE_PEERS = [(k, d) for d in (0, 1, 3, 2) for k in (0, 1) if (k, d) != (0, 0)]
PLANE = [(a, b) for a in range(4) for b in range(4) if (a, b) != (0, 0)]
C_PEERS = [(a, b) for a in (0, 2) for b in range(4) if (a, b) != (0, 0)]


def place():
    rep, dp = lax.axis_index("replica"), lax.axis_index("dp")
    return dp // 8, lax.rem(dp // 2, 4), lax.rem(dp, 2), rep // 2, lax.rem(rep, 2)


def at(z, x, y, c):
    return {"replica": lax.rem(y, 2) * 2 + c, "dp": z * 8 + x * 2 + y // 2}


def up(v, d):
    return lax.rem(v + d, 4)


def times_transposed(a, b):
    return lax.dot_general(a, b, (((1,), (1,)), ((), ())), preferred_element_type=f32)


def center(
    feat_ref,
    proto_ref,
    gath,
    c_out,
    r_out,
    f_out,
    F,
    W,
    K,
    cm,
    rm,
    csend,
    crecv,
    rpart,
    rs_recv,
    ysend,
    yz_recv,
    rfull,
    c_all,
    feat_sem,
    twin_sem,
    xg_sem,
    zb_sem,
    ya_sem,
    yb_sem,
    xa_sem,
    za_sem,
    xb_sem,
    col_sem,
    half_sem,
    yz_sem,
    full_sem,
    call_sem,
    local_sem,
):
    z, x, h, l, c = place()
    y = h * 2 + l
    m0 = z * 2 + h
    xp, xm, xo = at(z, up(x, 1), y, c), at(z, up(x, 3), y, c), up(x, 2)
    zp, zm = at(up(z, 1), x, y, c), at(up(z, 3), x, y, c)
    twin = at(z, x, y, 1 - c)
    yo = at(z, x, up(y, 2), c)

    barrier = pltpu.get_barrier_semaphore()
    peers = [at(z, up(x, d), y, c) for d in (1, 2, 3)]
    peers += [at(up(z, b), x, up(y, a), c) for a, b in PLANE] + [twin]
    for p in peers:
        pl.semaphore_signal(barrier, inc=1, device_id=p, device_id_type=pl.DeviceIdType.MESH)

    fv = feat_ref[...].astype(f32)
    fn = (fv * lax.rsqrt(jnp.sum(fv * fv, axis=1, keepdims=True) + epsilon)).astype(bf16)
    f_out[...] = fn
    F[pl.ds(pl.multiple_of(m0 * 384, 384), 384), :] = fn
    pv = proto_ref[...].astype(f32)
    W[x] = (pv * lax.rsqrt(jnp.sum(pv * pv, axis=0, keepdims=True) + epsilon)).astype(bf16)

    pl.semaphore_wait(barrier, len(peers))
    sends = []

    def remote(src, dst, sems, idx, dev):
        return pltpu.make_async_remote_copy(
            src_ref=src,
            dst_ref=dst,
            send_sem=sems.at[0, idx],
            recv_sem=sems.at[1, idx],
            device_id=dev,
            device_id_type=pl.DeviceIdType.MESH,
        )

    def send(src, dst, sems, idx, dev):
        cp = remote(src, dst, sems, idx, dev)
        cp.start()
        sends.append(cp)

    def arrived(ref, sems, idx):
        remote(ref, ref, sems, idx, twin).wait_recv()

    def g(zz, xx, hh, lo, n):
        return gath.at[zz * 8 + xx * 2 + hh, pl.ds(lo, n)]

    def xh(xx, k):
        return W.at[xx, pl.ds(k * 128, 128)]

    send(xh(x, 0), xh(x, 0), xg_sem, 0, xp)
    send(xh(x, 1), xh(x, 1), xg_sem, 2, xm)
    send(xh(x, 1), xh(x, 1), xg_sem, 1, xp)
    send(xh(x, 0), xh(x, 0), xg_sem, 3, xm)

    def fpart(zz, hh, cc):
        return F.at[pl.ds(pl.multiple_of((zz * 2 + hh) * 384 + cc * 192, 64), 192)]

    mine = fpart(z, h, c)
    for i, (k, d) in enumerate(FEATURE_PEERS):
        send(mine, mine, feat_sem, i, at(up(z, d), x, 3 - y if k else y, c))

    def zq(zz, hh, q):
        return g(zz, x, hh, 128 + q * 64, 64)

    def wq(q):
        return W.at[x, pl.ds(128 + q * 64, 64)]

    send(wq(0), zq(z, h, 0), zb_sem, 0, zp)
    send(wq(1), zq(z, h, 1), zb_sem, 2, zm)
    send(wq(1), zq(z, h, 1), zb_sem, 1, zp)
    send(wq(0), zq(z, h, 0), zb_sem, 3, zm)

    locals_ = []

    def keep(xx, i):
        cp = pltpu.make_async_copy(W.at[xx], gath.at[z * 8 + xx * 2 + h], local_sem.at[i])
        cp.start()
        locals_.append(cp)

    keep(x, 0)

    def b_forward():
        arrived(zq(up(z, 3), h, 0), zb_sem, 0)
        send(zq(up(z, 3), h, 0), zq(up(z, 3), h, 0), zb_sem, 4, zp)
        arrived(zq(up(z, 1), h, 1), zb_sem, 2)
        send(zq(up(z, 1), h, 1), zq(up(z, 1), h, 1), zb_sem, 5, zm)

    def b2():
        arrived(hb(z, x, 1 - h), yb_sem, 0)
        for q, i, dev in ((0, 0, zp), (1, 2, zm), (1, 1, zp), (0, 3, zm)):
            send(zq(z, 1 - h, q), zq(z, 1 - h, q), zb_sem, 6 + i, dev)

    def b2_forward():
        arrived(zq(up(z, 3), 1 - h, 0), zb_sem, 6)
        send(zq(up(z, 3), 1 - h, 0), zq(up(z, 3), 1 - h, 0), zb_sem, 10, zp)
        arrived(zq(up(z, 1), 1 - h, 1), zb_sem, 8)
        send(zq(up(z, 1), 1 - h, 1), zq(up(z, 1), 1 - h, 1), zb_sem, 11, zm)

    def hb(zz, xx, hh):
        return g(zz, xx, hh, 128, 128)

    def ha(zz, xx, hh):
        return g(zz, xx, hh, 0, 128)

    def yb0():
        send(W.at[x, pl.ds(128, 128)], hb(z, x, h), yb_sem, 0, yo)

    def b_rest(o):
        hh, k = (1 - h, 6) if o else (h, 0)
        arrived(zq(up(z, 3), hh, 1), zb_sem, k + 1)
        arrived(zq(up(z, 1), hh, 0), zb_sem, k + 3)
        arrived(zq(up(z, 2), hh, 0), zb_sem, k + 4)
        arrived(zq(up(z, 2), hh, 1), zb_sem, k + 5)

    def ya0():
        send(W.at[x, pl.ds(0, 128)], ha(z, x, h), ya_sem, 0, yo)

    def za_ref(zz, i):
        return ha(zz, up(x, DX[i % 4]), h if i < 4 else 1 - h)

    def za(i):
        if i >= 4:
            src = za_ref(z, i)
        else:
            src = W.at[up(x, DX[i]), pl.ds(0, 128)]
        send(src, za_ref(z, i), za_sem, i, zp)
        send(src, za_ref(z, i), za_sem, 8 + i, zm)

    def za_forward(i):
        lo, hi = za_ref(up(z, 3), i), za_ref(up(z, 1), i)
        if i % 2 == 0:
            arrived(lo, za_sem, i)
            send(lo, lo, za_sem, 16 + i, zp)
        else:
            arrived(hi, za_sem, 8 + i)
            send(hi, hi, za_sem, 16 + i, zm)

    XB = [(1, 0), (3, 0), (2, 0), (0, 1), (1, 1), (3, 1), (2, 1)]

    def xb_ref(xx, j):
        d, o = XB[j]
        return hb(up(z, d), xx, 1 - h if o else h)

    def xb(j):
        send(xb_ref(x, j), xb_ref(x, j), xb_sem, j, xp)
        send(xb_ref(x, j), xb_ref(x, j), xb_sem, 7 + j, xm)

    def xb_forward(j):
        lo, hi = xb_ref(up(x, 3), j), xb_ref(up(x, 1), j)
        if j % 2 == 0:
            arrived(lo, xb_sem, j)
            send(lo, lo, xb_sem, 14 + j, xp)
        else:
            arrived(hi, xb_sem, 7 + j)
            send(hi, hi, xb_sem, 14 + j, xm)

    def xb_rest(j):
        if j % 2 == 0:
            arrived(xb_ref(up(x, 1), j), xb_sem, 7 + j)
        else:
            arrived(xb_ref(up(x, 3), j), xb_sem, j)
        arrived(xb_ref(up(x, 2), j), xb_sem, 14 + j)

    def aq(xx, q):
        return g(z, xx, 1 - h, q * 64, 64)

    def xa():
        arrived(ha(z, x, 1 - h), ya_sem, 0)
        for q, i, dev in ((0, 0, xp), (1, 2, xm), (1, 1, xp), (0, 3, xm)):
            send(aq(x, q), aq(x, q), xa_sem, i, dev)

    def xa_forward():
        arrived(aq(up(x, 3), 0), xa_sem, 0)
        send(aq(up(x, 3), 0), aq(up(x, 3), 0), xa_sem, 4, xp)
        arrived(aq(up(x, 1), 1), xa_sem, 2)
        send(aq(up(x, 1), 1), aq(up(x, 1), 1), xa_sem, 5, xm)

    def xa_rest():
        arrived(aq(up(x, 3), 1), xa_sem, 1)
        arrived(aq(up(x, 1), 0), xa_sem, 3)
        arrived(aq(xo, 0), xa_sem, 4)
        arrived(aq(xo, 1), xa_sem, 5)

    def near(i):
        if i % 2 == 0:
            arrived(za_ref(up(z, 1), i), za_sem, 8 + i)
        else:
            arrived(za_ref(up(z, 3), i), za_sem, i)

    def far(i):
        arrived(za_ref(up(z, 2), i), za_sem, 16 + i)

    def many(fn, ids):
        return [functools.partial(fn, i) for i in ids]

    plan = {
        "start": [yb0, ya0] + many(za, (0,)),
        "k0": [b_forward, b2],
        "k3": [xa],
        "k1": many(za, (1,)),
        "k2": many(za, (2, 3)) + many(b_rest, (0,)) + many(xb, (0,)),
        "colx0": [xa_forward] + many(xb, (1, 2)) + [b2_forward],
        "mid0": many(xb_forward, (0,)),
        "yz0": many(za_forward, (0, 1)) + many(b_rest, (1,)) + [xa_rest] + many(za, (4, 5)),
        "colx1": many(xb_forward, (1,)) + many(xb, (3, 4)),
        "mid1": many(xb_forward, (2,)),
        "yz1": many(za_forward, (2, 3)) + many(za, (6, 7)),
        "col2": many(za_forward, (4,)),
        "colx2": many(xb_forward, (3,)) + many(xb, (5, 6)),
        "mid2": many(xb_forward, (4,)),
        "yz2": many(za_forward, (5, 6, 7)) + many(xb_forward, (5, 6)),
        "rest": many(near, range(8)) + many(far, range(8)) + many(xb_rest, range(7)),
    }

    def run(point):
        for fn in plan.pop(point, ()):
            fn()

    def exponentials(d):
        xx = up(x, d)
        w = W.at[xx]

        def body(rb, acc):
            r0 = pl.multiple_of(rb * 1024, 1024)
            a = F[pl.ds(r0, 1024), :]
            parts = []
            for q in range(4):
                s = jnp.dot(a, w[:, q * 256 : (q + 1) * 256], preferred_element_type=f32)
                e = jnp.exp2(s * log2_scale)
                c0 = pl.multiple_of(xx * 1024 + q * 256, 256)
                K[pl.ds(r0, 1024), pl.ds(c0, 256)] = e.astype(bf16)
                parts.append(jnp.sum(e.reshape(128, 8, 256), axis=0))
            return acc + jnp.concatenate(parts, axis=1)

        acc = lax.fori_loop(0, ROWS // 1024, body, jnp.zeros((8, 1024), f32))
        csend[0, xx] = jnp.sum(acc, axis=0, keepdims=True)

    run("start")
    arrived(xh(up(x, 3), 0), xg_sem, 0)
    send(xh(up(x, 3), 0), xh(up(x, 3), 0), xg_sem, 4, xp)
    arrived(xh(up(x, 1), 1), xg_sem, 2)
    send(xh(up(x, 1), 1), xh(up(x, 1), 1), xg_sem, 5, xm)
    for i, (k, d) in enumerate(FEATURE_PEERS):
        part = fpart(up(z, 4 - d), 1 - h if k else h, c)
        arrived(part, feat_sem, i)
        send(part, part, twin_sem, i, twin)
    for i, (k, d) in enumerate(FEATURE_PEERS):
        arrived(fpart(up(z, 4 - d), 1 - h if k else h, 1 - c), twin_sem, i)
    exponentials(0)
    run("k0")
    arrived(xh(up(x, 3), 1), xg_sem, 1)
    keep(up(x, 3), 1)
    run("k3")
    exponentials(3)
    arrived(xh(up(x, 1), 0), xg_sem, 3)
    keep(up(x, 1), 2)
    run("k1")
    exponentials(1)
    arrived(xh(xo, 0), xg_sem, 4)
    arrived(xh(xo, 1), xg_sem, 5)
    keep(xo, 3)
    run("k2")
    exponentials(2)

    for t in range(ITERS):
        if t:
            run("col%d" % t)
            for hf in range(2):
                s = jnp.dot(rm[...], K[:, hf * 2048 : (hf + 1) * 2048], preferred_element_type=f32)
                csend[t, 2 * hf] = s[0:1, 0:1024]
                csend[t, 2 * hf + 1] = s[0:1, 1024:2048]
        for d in (1, 2, 3):
            send(csend.at[t], crecv.at[t, d - 1], col_sem, t * 3 + d - 1, at(z, up(x, d), y, c))
        run("colx%d" % t)
        for d in (1, 2, 3):
            arrived(crecv.at[t, d - 1], col_sem, t * 3 + d - 1)
        cols = 1.0 / (csend[t] + crecv[t, 0] + crecv[t, 1] + crecv[t, 2])
        for u in range(4):
            cm[:, u * 1024 : (u + 1) * 1024] = jnp.broadcast_to(cols[u], (16, 1024)).astype(bf16)
        if t == ITERS - 1:
            c_all[m0] = cols
            for i, (a, b) in enumerate(C_PEERS):
                send(c_all.at[m0], c_all.at[m0], call_sem, i, at(up(z, b), x, up(y, a), c))

        for hf in range(2):
            if hf:
                run("mid%d" % t)

            @pl.loop(0, 3)
            def _(rb):
                r0 = pl.multiple_of(rb * 512, 512)
                k0 = pl.multiple_of(hf * 1536 + rb * 512, 512)
                s = times_transposed(cm[:, :SPLIT], K[pl.ds(k0, 512), :SPLIT])
                sums = []
                for b in range(8):
                    acc = jnp.zeros((64, 128), f32)
                    for j in range(SPLIT, COLS, 128):
                        kk = K[pl.ds(k0 + b * 64, 64), j : j + 128].astype(f32)
                        acc = acc + kk * jnp.tile(cm[:, j : j + 128], (4, 1)).astype(f32)
                    sums.append(acc)
                acc = jnp.concatenate(sums, axis=0)
                hi = acc.astype(bf16)
                lo = (acc - hi.astype(f32)).astype(bf16)
                ones = jnp.ones((16, 128), bf16)
                s = s + times_transposed(ones, hi) + times_transposed(ones, lo)
                rpart[t, hf, :, pl.ds(r0, 512)] = s[0:1]

        send(rpart.at[t, 1 - c], rs_recv.at[t], half_sem, t, twin)
        arrived(rs_recv.at[t], half_sem, t)
        ysend[t] = rpart[t, c] + rs_recv[t]
        for i, (a, b) in enumerate(PLANE):
            send(ysend.at[t], yz_recv.at[t, i], yz_sem, t * 15 + i, at(up(z, b), x, up(y, a), c))
        run("yz%d" % t)
        for i in range(15):
            arrived(yz_recv.at[t, i], yz_sem, t * 15 + i)
        total = ysend[t] + jnp.sum(yz_recv[t], axis=0)
        rfull[t, c] = 1.0 / total
        send(rfull.at[t, c], rfull.at[t, c], full_sem, t, twin)
        arrived(rfull.at[t, 1 - c], full_sem, t)
        if t < ITERS - 1:
            for hf in range(2):
                rm[:, hf * 1536 : (hf + 1) * 1536] = jnp.broadcast_to(rfull[t, hf], (16, 1536)).astype(bf16)

    r_out[...] = rfull[ITERS - 1, m0 // 4, :, pl.ds(pl.multiple_of(lax.rem(m0, 4) * 384, 384), 384)]
    run("rest")
    for i, (a, b) in enumerate(C_PEERS):
        arrived(c_all.at[up(z, 4 - b) * 2 + up(y, 4 - a) // 2], call_sem, i)
    c_out[...] = c_all[...]
    for cp in locals_:
        cp.wait()
    for cp in sends:
        cp.wait_send()


NB = 4


def finish(f_ref, w_ref, r_ref, c_ref, o_ref, rcol, wb, ob, si, so):
    def fetch(i, s):
        return pltpu.make_async_copy(w_ref.at[i], wb.at[s], si.at[s])

    def write(i, s):
        cols = pl.ds(pl.multiple_of(i * 1024, 1024), 1024)
        return pltpu.make_async_copy(ob.at[s], o_ref.at[:, cols], so.at[s])

    for s in range(NB - 1):
        fetch(s, s).start()
    rcol[...] = jnp.broadcast_to(r_ref[...] * PROTOS, (8, 384)).T

    @pl.loop(0, 32)
    def _(i):
        s = lax.rem(i, NB)

        @pl.when(i + NB - 1 < 32)
        def _():
            fetch(i + NB - 1, lax.rem(i + NB - 1, NB)).start()

        fetch(i, s).wait()

        @pl.when(i >= NB)
        def _():
            write(i - NB, s).wait()

        cols = c_ref[(i // 8) * 2 + lax.rem(i, 2), lax.rem(i // 2, 4)]
        for rb in range(3):
            rows = slice(rb * 128, (rb + 1) * 128)
            sc = jnp.dot(f_ref[rows, :], wb[s], preferred_element_type=f32)
            ob[s, rows, :] = (jnp.exp2(sc * log2_scale) * rcol[rows, 0:1] * cols).astype(bf16)
        write(i, s).start()

    for i in range(32 - NB, 32):
        write(i, i % NB).wait()


def local(features, prototypes):
    vmem, anywhere = pl.BlockSpec(memory_space=pltpu.VMEM), pl.BlockSpec(memory_space=pl.ANY)
    dma = lambda n: pltpu.SemaphoreType.DMA((2, n))
    gathered, cols, rows, normed = pl.pallas_call(
        center,
        name="center",
        out_shape=(
            jax.ShapeDtypeStruct((32, 256, 1024), bf16),
            jax.ShapeDtypeStruct((8, 4, 1, 1024), f32),
            jax.ShapeDtypeStruct((1, 384), f32),
            jax.ShapeDtypeStruct((384, 256), bf16),
        ),
        in_specs=[vmem, vmem],
        out_specs=(anywhere, vmem, vmem, vmem),
        scratch_shapes=[
            pltpu.VMEM((ROWS, 256), bf16),
            pltpu.VMEM((4, 256, 1024), bf16),
            pltpu.VMEM((ROWS, COLS), bf16),
            pltpu.VMEM((16, COLS), bf16),
            pltpu.VMEM((16, ROWS), bf16),
            pltpu.VMEM((ITERS, 4, 1, 1024), f32),
            pltpu.VMEM((ITERS, 3, 4, 1, 1024), f32),
            pltpu.VMEM((ITERS, 2, 1, 1536), f32),
            pltpu.VMEM((ITERS, 1, 1536), f32),
            pltpu.VMEM((ITERS, 1, 1536), f32),
            pltpu.VMEM((ITERS, 15, 1, 1536), f32),
            pltpu.VMEM((ITERS, 2, 1, 1536), f32),
            pltpu.VMEM((8, 4, 1, 1024), f32),
            dma(7),
            dma(7),
            dma(6),
            dma(12),
            dma(1),
            dma(1),
            dma(6),
            dma(24),
            dma(21),
            dma(9),
            dma(3),
            dma(45),
            dma(3),
            dma(7),
            pltpu.SemaphoreType.DMA((4,)),
        ],
        compiler_params=pltpu.CompilerParams(
            collective_id=0, has_side_effects=True, vmem_limit_bytes=56 << 20
        ),
    )(features, prototypes)
    return pl.pallas_call(
        finish,
        name="finish",
        out_shape=jax.ShapeDtypeStruct((384, 32768), bf16),
        in_specs=[vmem, anywhere, vmem, vmem],
        out_specs=anywhere,
        scratch_shapes=[
            pltpu.VMEM((384, 8), f32),
            pltpu.VMEM((NB, 256, 1024), bf16),
            pltpu.VMEM((NB, 384, 1024), bf16),
            pltpu.SemaphoreType.DMA((NB,)),
            pltpu.SemaphoreType.DMA((NB,)),
        ],
        compiler_params=pltpu.CompilerParams(vmem_limit_bytes=56 << 20),
    )(normed, gathered, rows, cols)


def solution(mesh):
    placed = (P("dp", None), P(None, ("replica", "dp")))
    return jax.shard_map(
        local, mesh=mesh, in_specs=placed, out_specs=P("dp", "replica"), check_vma=False
    )
```

```python
import functools

import jax
import jax.numpy as jnp
from jax import lax
from jax.experimental import pallas as pl
from jax.experimental.pallas import tpu as pltpu
from jax.sharding import PartitionSpec as P

PROTOS = 131072
ITERS = 3
epsilon = 1e-06
log2_scale = 1.4426950408889634 / 0.07

f32, bf16 = jnp.float32, jnp.bfloat16
ROWS, COLS = 3072, 4096
SPLIT = 2304
DX = (0, 1, 3, 2)
FEATURE_PEERS = [(k, d) for d in (0, 1, 3, 2) for k in (0, 1) if (k, d) != (0, 0)]
PLANE = [(a, b) for a in range(4) for b in range(4) if (a, b) != (0, 0)]
C_PEERS = [(a, b) for a in (0, 2) for b in range(4) if (a, b) != (0, 0)]


def place():
    rep, dp = lax.axis_index("replica"), lax.axis_index("dp")
    return dp // 8, lax.rem(dp // 2, 4), lax.rem(dp, 2), rep // 2, lax.rem(rep, 2)


def at(z, x, y, c):
    return {"replica": lax.rem(y, 2) * 2 + c, "dp": z * 8 + x * 2 + y // 2}


def up(v, d):
    return lax.rem(v + d, 4)


def times_transposed(a, b):
    return lax.dot_general(a, b, (((1,), (1,)), ((), ())), preferred_element_type=f32)


def center(
    feat_ref,
    proto_ref,
    gath,
    c_out,
    r_out,
    f_out,
    F,
    W,
    K,
    cm,
    rm,
    csend,
    crecv,
    rpart,
    rs_recv,
    ysend,
    yz_recv,
    rfull,
    c_all,
    feat_sem,
    twin_sem,
    xg_sem,
    zb_sem,
    ya_sem,
    yb_sem,
    xa_sem,
    za_sem,
    xb_sem,
    col_sem,
    half_sem,
    yz_sem,
    full_sem,
    call_sem,
    local_sem,
):
    z, x, h, l, c = place()
    y = h * 2 + l
    m0 = z * 2 + h
    xp, xm, xo = at(z, up(x, 1), y, c), at(z, up(x, 3), y, c), up(x, 2)
    zp, zm = at(up(z, 1), x, y, c), at(up(z, 3), x, y, c)
    twin = at(z, x, y, 1 - c)
    yo = at(z, x, up(y, 2), c)

    barrier = pltpu.get_barrier_semaphore()
    peers = [at(z, up(x, d), y, c) for d in (1, 2, 3)]
    peers += [at(up(z, b), x, up(y, a), c) for a, b in PLANE] + [twin]
    for p in peers:
        pl.semaphore_signal(barrier, inc=1, device_id=p, device_id_type=pl.DeviceIdType.MESH)

    fv = feat_ref[...].astype(f32)
    fn = (fv * lax.rsqrt(jnp.sum(fv * fv, axis=1, keepdims=True) + epsilon)).astype(bf16)
    f_out[...] = fn
    F[pl.ds(pl.multiple_of(m0 * 384, 384), 384), :] = fn
    pv = proto_ref[...].astype(f32)
    W[x] = (pv * lax.rsqrt(jnp.sum(pv * pv, axis=0, keepdims=True) + epsilon)).astype(bf16)

    pl.semaphore_wait(barrier, len(peers))
    sends = []

    def remote(src, dst, sems, idx, dev):
        return pltpu.make_async_remote_copy(
            src_ref=src,
            dst_ref=dst,
            send_sem=sems.at[0, idx],
            recv_sem=sems.at[1, idx],
            device_id=dev,
            device_id_type=pl.DeviceIdType.MESH,
        )

    def send(src, dst, sems, idx, dev):
        cp = remote(src, dst, sems, idx, dev)
        cp.start()
        sends.append(cp)

    def arrived(ref, sems, idx):
        remote(ref, ref, sems, idx, twin).wait_recv()

    def g(zz, xx, hh, lo, n):
        return gath.at[zz * 8 + xx * 2 + hh, pl.ds(lo, n)]

    def xh(xx, k):
        return W.at[xx, pl.ds(k * 128, 128)]

    send(xh(x, 0), xh(x, 0), xg_sem, 0, xp)
    send(xh(x, 1), xh(x, 1), xg_sem, 2, xm)
    send(xh(x, 1), xh(x, 1), xg_sem, 1, xp)
    send(xh(x, 0), xh(x, 0), xg_sem, 3, xm)

    def fpart(zz, hh, cc):
        return F.at[pl.ds(pl.multiple_of((zz * 2 + hh) * 384 + cc * 192, 64), 192)]

    mine = fpart(z, h, c)
    for i, (k, d) in enumerate(FEATURE_PEERS):
        send(mine, mine, feat_sem, i, at(up(z, d), x, 3 - y if k else y, c))

    def zq(zz, hh, q):
        return g(zz, x, hh, 128 + q * 64, 64)

    def wq(q):
        return W.at[x, pl.ds(128 + q * 64, 64)]

    send(wq(0), zq(z, h, 0), zb_sem, 0, zp)
    send(wq(1), zq(z, h, 1), zb_sem, 2, zm)
    send(wq(1), zq(z, h, 1), zb_sem, 1, zp)
    send(wq(0), zq(z, h, 0), zb_sem, 3, zm)

    locals_ = []

    def keep(xx, i):
        cp = pltpu.make_async_copy(W.at[xx], gath.at[z * 8 + xx * 2 + h], local_sem.at[i])
        cp.start()
        locals_.append(cp)

    keep(x, 0)

    def b_forward():
        arrived(zq(up(z, 3), h, 0), zb_sem, 0)
        send(zq(up(z, 3), h, 0), zq(up(z, 3), h, 0), zb_sem, 4, zp)
        arrived(zq(up(z, 1), h, 1), zb_sem, 2)
        send(zq(up(z, 1), h, 1), zq(up(z, 1), h, 1), zb_sem, 5, zm)

    def b2():
        arrived(hb(z, x, 1 - h), yb_sem, 0)
        for q, i, dev in ((0, 0, zp), (1, 2, zm), (1, 1, zp), (0, 3, zm)):
            send(zq(z, 1 - h, q), zq(z, 1 - h, q), zb_sem, 6 + i, dev)

    def b2_forward():
        arrived(zq(up(z, 3), 1 - h, 0), zb_sem, 6)
        send(zq(up(z, 3), 1 - h, 0), zq(up(z, 3), 1 - h, 0), zb_sem, 10, zp)
        arrived(zq(up(z, 1), 1 - h, 1), zb_sem, 8)
        send(zq(up(z, 1), 1 - h, 1), zq(up(z, 1), 1 - h, 1), zb_sem, 11, zm)

    def hb(zz, xx, hh):
        return g(zz, xx, hh, 128, 128)

    def ha(zz, xx, hh):
        return g(zz, xx, hh, 0, 128)

    def yb0():
        send(W.at[x, pl.ds(128, 128)], hb(z, x, h), yb_sem, 0, yo)

    def b_rest(o):
        hh, k = (1 - h, 6) if o else (h, 0)
        arrived(zq(up(z, 3), hh, 1), zb_sem, k + 1)
        arrived(zq(up(z, 1), hh, 0), zb_sem, k + 3)
        arrived(zq(up(z, 2), hh, 0), zb_sem, k + 4)
        arrived(zq(up(z, 2), hh, 1), zb_sem, k + 5)

    def ya0():
        send(W.at[x, pl.ds(0, 128)], ha(z, x, h), ya_sem, 0, yo)

    def za_ref(zz, i):
        return ha(zz, up(x, DX[i % 4]), h if i < 4 else 1 - h)

    def za(i):
        if i >= 4:
            src = za_ref(z, i)
        else:
            src = W.at[up(x, DX[i]), pl.ds(0, 128)]
        send(src, za_ref(z, i), za_sem, i, zp)
        send(src, za_ref(z, i), za_sem, 8 + i, zm)

    def za_forward(i):
        lo, hi = za_ref(up(z, 3), i), za_ref(up(z, 1), i)
        if i % 2 == 0:
            arrived(lo, za_sem, i)
            send(lo, lo, za_sem, 16 + i, zp)
        else:
            arrived(hi, za_sem, 8 + i)
            send(hi, hi, za_sem, 16 + i, zm)

    XB = [(1, 0), (3, 0), (2, 0), (0, 1), (1, 1), (3, 1), (2, 1)]

    def xb_ref(xx, j):
        d, o = XB[j]
        return hb(up(z, d), xx, 1 - h if o else h)

    def xb(j):
        send(xb_ref(x, j), xb_ref(x, j), xb_sem, j, xp)
        send(xb_ref(x, j), xb_ref(x, j), xb_sem, 7 + j, xm)

    def xb_forward(j):
        lo, hi = xb_ref(up(x, 3), j), xb_ref(up(x, 1), j)
        if j % 2 == 0:
            arrived(lo, xb_sem, j)
            send(lo, lo, xb_sem, 14 + j, xp)
        else:
            arrived(hi, xb_sem, 7 + j)
            send(hi, hi, xb_sem, 14 + j, xm)

    def xb_rest(j):
        if j % 2 == 0:
            arrived(xb_ref(up(x, 1), j), xb_sem, 7 + j)
        else:
            arrived(xb_ref(up(x, 3), j), xb_sem, j)
        arrived(xb_ref(up(x, 2), j), xb_sem, 14 + j)

    def aq(xx, q):
        return g(z, xx, 1 - h, q * 64, 64)

    def xa():
        arrived(ha(z, x, 1 - h), ya_sem, 0)
        for q, i, dev in ((0, 0, xp), (1, 2, xm), (1, 1, xp), (0, 3, xm)):
            send(aq(x, q), aq(x, q), xa_sem, i, dev)

    def xa_forward():
        arrived(aq(up(x, 3), 0), xa_sem, 0)
        send(aq(up(x, 3), 0), aq(up(x, 3), 0), xa_sem, 4, xp)
        arrived(aq(up(x, 1), 1), xa_sem, 2)
        send(aq(up(x, 1), 1), aq(up(x, 1), 1), xa_sem, 5, xm)

    def xa_rest():
        arrived(aq(up(x, 3), 1), xa_sem, 1)
        arrived(aq(up(x, 1), 0), xa_sem, 3)
        arrived(aq(xo, 0), xa_sem, 4)
        arrived(aq(xo, 1), xa_sem, 5)

    def near(i):
        if i % 2 == 0:
            arrived(za_ref(up(z, 1), i), za_sem, 8 + i)
        else:
            arrived(za_ref(up(z, 3), i), za_sem, i)

    def far(i):
        arrived(za_ref(up(z, 2), i), za_sem, 16 + i)

    def many(fn, ids):
        return [functools.partial(fn, i) for i in ids]

    plan = {
        "start": [yb0, ya0] + many(za, (0,)),
        "k0": [b_forward, b2],
        "k3": [xa],
        "k1": many(za, (1,)),
        "k2": many(za, (2, 3)) + many(b_rest, (0,)) + many(xb, (0,)),
        "colx0": [xa_forward] + many(xb, (1, 2)) + [b2_forward],
        "mid0": many(xb_forward, (0,)),
        "yz0": many(za_forward, (0, 1)) + many(b_rest, (1,)) + [xa_rest] + many(za, (4, 5)),
        "colx1": many(xb_forward, (1,)) + many(xb, (3, 4)),
        "mid1": many(xb_forward, (2,)),
        "yz1": many(za_forward, (2, 3)) + many(za, (6, 7)),
        "col2": many(za_forward, (4,)),
        "colx2": many(xb_forward, (3,)) + many(xb, (5, 6)),
        "mid2": many(xb_forward, (4,)),
        "yz2": many(xb_forward, (5,)) + many(za_forward, (5,)) + many(xb_forward, (6,)) + many(za_forward, (6, 7)),
        "rest": many(near, range(8)) + many(far, range(8)) + many(xb_rest, range(7)),
    }

    def run(point):
        for fn in plan.pop(point, ()):
            fn()

    def exponentials(d):
        xx = up(x, d)
        w = W.at[xx]

        def body(rb, acc):
            r0 = pl.multiple_of(rb * 1024, 1024)
            a = F[pl.ds(r0, 1024), :]
            parts = []
            for q in range(4):
                s = jnp.dot(a, w[:, q * 256 : (q + 1) * 256], preferred_element_type=f32)
                e = jnp.exp2(s * log2_scale)
                c0 = pl.multiple_of(xx * 1024 + q * 256, 256)
                K[pl.ds(r0, 1024), pl.ds(c0, 256)] = e.astype(bf16)
                parts.append(jnp.sum(e.reshape(128, 8, 256), axis=0))
            return acc + jnp.concatenate(parts, axis=1)

        acc = lax.fori_loop(0, ROWS // 1024, body, jnp.zeros((8, 1024), f32))
        csend[0, xx] = jnp.sum(acc, axis=0, keepdims=True)

    run("start")
    arrived(xh(up(x, 3), 0), xg_sem, 0)
    send(xh(up(x, 3), 0), xh(up(x, 3), 0), xg_sem, 4, xp)
    arrived(xh(up(x, 1), 1), xg_sem, 2)
    send(xh(up(x, 1), 1), xh(up(x, 1), 1), xg_sem, 5, xm)
    for i, (k, d) in enumerate(FEATURE_PEERS):
        part = fpart(up(z, 4 - d), 1 - h if k else h, c)
        arrived(part, feat_sem, i)
        send(part, part, twin_sem, i, twin)
    for i, (k, d) in enumerate(FEATURE_PEERS):
        arrived(fpart(up(z, 4 - d), 1 - h if k else h, 1 - c), twin_sem, i)
    exponentials(0)
    run("k0")
    arrived(xh(up(x, 3), 1), xg_sem, 1)
    keep(up(x, 3), 1)
    run("k3")
    exponentials(3)
    arrived(xh(up(x, 1), 0), xg_sem, 3)
    keep(up(x, 1), 2)
    run("k1")
    exponentials(1)
    arrived(xh(xo, 0), xg_sem, 4)
    arrived(xh(xo, 1), xg_sem, 5)
    keep(xo, 3)
    run("k2")
    exponentials(2)

    for t in range(ITERS):
        if t:
            run("col%d" % t)
            for hf in range(2):
                s = jnp.dot(rm[...], K[:, hf * 2048 : (hf + 1) * 2048], preferred_element_type=f32)
                csend[t, 2 * hf] = s[0:1, 0:1024]
                csend[t, 2 * hf + 1] = s[0:1, 1024:2048]
        for d in (1, 2, 3):
            send(csend.at[t], crecv.at[t, d - 1], col_sem, t * 3 + d - 1, at(z, up(x, d), y, c))
        run("colx%d" % t)
        for d in (1, 2, 3):
            arrived(crecv.at[t, d - 1], col_sem, t * 3 + d - 1)
        cols = 1.0 / (csend[t] + crecv[t, 0] + crecv[t, 1] + crecv[t, 2])
        for u in range(4):
            cm[:, u * 1024 : (u + 1) * 1024] = jnp.broadcast_to(cols[u], (16, 1024)).astype(bf16)
        if t == ITERS - 1:
            c_all[m0] = cols
            for i, (a, b) in enumerate(C_PEERS):
                send(c_all.at[m0], c_all.at[m0], call_sem, i, at(up(z, b), x, up(y, a), c))

        for hf in range(2):
            if hf:
                run("mid%d" % t)

            @pl.loop(0, 3)
            def _(rb):
                r0 = pl.multiple_of(rb * 512, 512)
                k0 = pl.multiple_of(hf * 1536 + rb * 512, 512)
                s = times_transposed(cm[:, :SPLIT], K[pl.ds(k0, 512), :SPLIT])
                sums = []
                for b in range(8):
                    acc = jnp.zeros((64, 128), f32)
                    for j in range(SPLIT, COLS, 128):
                        kk = K[pl.ds(k0 + b * 64, 64), j : j + 128].astype(f32)
                        acc = acc + kk * jnp.tile(cm[:, j : j + 128], (4, 1)).astype(f32)
                    sums.append(acc)
                acc = jnp.concatenate(sums, axis=0)
                hi = acc.astype(bf16)
                lo = (acc - hi.astype(f32)).astype(bf16)
                ones = jnp.ones((16, 128), bf16)
                s = s + times_transposed(ones, hi) + times_transposed(ones, lo)
                rpart[t, hf, :, pl.ds(r0, 512)] = s[0:1]

        send(rpart.at[t, 1 - c], rs_recv.at[t], half_sem, t, twin)
        arrived(rs_recv.at[t], half_sem, t)
        ysend[t] = rpart[t, c] + rs_recv[t]
        for i, (a, b) in enumerate(PLANE):
            send(ysend.at[t], yz_recv.at[t, i], yz_sem, t * 15 + i, at(up(z, b), x, up(y, a), c))
        run("yz%d" % t)
        for i in range(15):
            arrived(yz_recv.at[t, i], yz_sem, t * 15 + i)
        total = ysend[t] + jnp.sum(yz_recv[t], axis=0)
        rfull[t, c] = 1.0 / total
        send(rfull.at[t, c], rfull.at[t, c], full_sem, t, twin)
        arrived(rfull.at[t, 1 - c], full_sem, t)
        if t < ITERS - 1:
            for hf in range(2):
                rm[:, hf * 1536 : (hf + 1) * 1536] = jnp.broadcast_to(rfull[t, hf], (16, 1536)).astype(bf16)

    r_out[...] = rfull[ITERS - 1, m0 // 4, :, pl.ds(pl.multiple_of(lax.rem(m0, 4) * 384, 384), 384)]
    run("rest")
    for i, (a, b) in enumerate(C_PEERS):
        arrived(c_all.at[up(z, 4 - b) * 2 + up(y, 4 - a) // 2], call_sem, i)
    c_out[...] = c_all[...]
    for cp in locals_:
        cp.wait()
    for cp in sends:
        cp.wait_send()


NB = 6


def finish(f_ref, w_ref, r_ref, c_ref, o_ref, rcol, wb, ob, si, so):
    def fetch(i, s):
        return pltpu.make_async_copy(w_ref.at[i], wb.at[s], si.at[s])

    def write(i, s):
        cols = pl.ds(pl.multiple_of(i * 1024, 1024), 1024)
        return pltpu.make_async_copy(ob.at[s], o_ref.at[:, cols], so.at[s])

    for s in range(NB - 1):
        fetch(s, s).start()
    rcol[...] = jnp.broadcast_to(r_ref[...] * PROTOS, (8, 384)).T

    @pl.loop(0, 32)
    def _(i):
        s = lax.rem(i, NB)

        @pl.when(i + NB - 1 < 32)
        def _():
            fetch(i + NB - 1, lax.rem(i + NB - 1, NB)).start()

        fetch(i, s).wait()

        @pl.when(i >= NB)
        def _():
            write(i - NB, s).wait()

        cols = c_ref[(i // 8) * 2 + lax.rem(i, 2), lax.rem(i // 2, 4)]
        for rb in range(3):
            rows = slice(rb * 128, (rb + 1) * 128)
            sc = jnp.dot(f_ref[rows, :], wb[s], preferred_element_type=f32)
            ob[s, rows, :] = (jnp.exp2(sc * log2_scale) * rcol[rows, 0:1] * cols).astype(bf16)
        write(i, s).start()

    for i in range(32 - NB, 32):
        write(i, i % NB).wait()


def local(features, prototypes):
    vmem, anywhere = pl.BlockSpec(memory_space=pltpu.VMEM), pl.BlockSpec(memory_space=pl.ANY)
    dma = lambda n: pltpu.SemaphoreType.DMA((2, n))
    gathered, cols, rows, normed = pl.pallas_call(
        center,
        name="center",
        out_shape=(
            jax.ShapeDtypeStruct((32, 256, 1024), bf16),
            jax.ShapeDtypeStruct((8, 4, 1, 1024), f32),
            jax.ShapeDtypeStruct((1, 384), f32),
            jax.ShapeDtypeStruct((384, 256), bf16),
        ),
        in_specs=[vmem, vmem],
        out_specs=(anywhere, vmem, vmem, vmem),
        scratch_shapes=[
            pltpu.VMEM((ROWS, 256), bf16),
            pltpu.VMEM((4, 256, 1024), bf16),
            pltpu.VMEM((ROWS, COLS), bf16),
            pltpu.VMEM((16, COLS), bf16),
            pltpu.VMEM((16, ROWS), bf16),
            pltpu.VMEM((ITERS, 4, 1, 1024), f32),
            pltpu.VMEM((ITERS, 3, 4, 1, 1024), f32),
            pltpu.VMEM((ITERS, 2, 1, 1536), f32),
            pltpu.VMEM((ITERS, 1, 1536), f32),
            pltpu.VMEM((ITERS, 1, 1536), f32),
            pltpu.VMEM((ITERS, 15, 1, 1536), f32),
            pltpu.VMEM((ITERS, 2, 1, 1536), f32),
            pltpu.VMEM((8, 4, 1, 1024), f32),
            dma(7),
            dma(7),
            dma(6),
            dma(12),
            dma(1),
            dma(1),
            dma(6),
            dma(24),
            dma(21),
            dma(9),
            dma(3),
            dma(45),
            dma(3),
            dma(7),
            pltpu.SemaphoreType.DMA((4,)),
        ],
        compiler_params=pltpu.CompilerParams(
            collective_id=0, has_side_effects=True, vmem_limit_bytes=56 << 20
        ),
    )(features, prototypes)
    return pl.pallas_call(
        finish,
        name="finish",
        out_shape=jax.ShapeDtypeStruct((384, 32768), bf16),
        in_specs=[vmem, anywhere, vmem, vmem],
        out_specs=anywhere,
        scratch_shapes=[
            pltpu.VMEM((384, 8), f32),
            pltpu.VMEM((NB, 256, 1024), bf16),
            pltpu.VMEM((NB, 384, 1024), bf16),
            pltpu.SemaphoreType.DMA((NB,)),
            pltpu.SemaphoreType.DMA((NB,)),
        ],
        compiler_params=pltpu.CompilerParams(vmem_limit_bytes=56 << 20),
    )(normed, gathered, rows, cols)


def solution(mesh):
    placed = (P("dp", None), P(None, ("replica", "dp")))
    return jax.shard_map(
        local, mesh=mesh, in_specs=placed, out_specs=P("dp", "replica"), check_vma=False
    )
```
